32 devices in a mesh: grp: 2 (over y), ctx: 4 (over z), kvh: 2 (over x), sub: 2 (over core).
Axes of the slice: x: 2, y: 2, z: 4, core: 2. Of those that a mesh axis runs over, the one named last changes fastest.
Arguments:
- queries: bfloat16 [1024, 8, 8, 128], P(('grp', 'ctx'), 'kvh', 'sub'), parts along dimension 0
- new_keys: bfloat16 [1024, 8, 128], P(('grp', 'ctx'), 'kvh'), parts along dimension 0
- new_values: bfloat16 [1024, 8, 128], P(('grp', 'ctx'), 'kvh'), parts along dimension 0, may hold values from -6 to 6
- cache_keys: bfloat16 [16384, 8, 128], P(('grp', 'ctx'), 'kvh'), parts along dimension 0, may hold values from -16 to 16
- cache_values: bfloat16 [16384, 8, 128], P(('grp', 'ctx'), 'kvh'), parts along dimension 0, may hold values from -6 to 6
- vertical_pool: int32 [16], P(('grp', 'ctx')), parts along dimension 0, may hold values from 0 to 15, as said below
- vertical_lists: int32 [8, 6], P(('grp', 'ctx')), parts along dimension 0, may hold values from 0 to 7, as said below
- slash_lists: int32 [8, 2], P(('grp', 'ctx')), parts along dimension 0, may hold values from 0 to 1, as said below
- list_counts: int32 [8, 2], P(('grp', 'ctx')), parts along dimension 0, may hold values from 1 to 6, as said below
Outputs:
- attention: bfloat16 [1024, 8, 8, 128], P(('grp', 'ctx'), 'kvh', 'sub'), parts along dimension 0
The draws below stay inside these ranges and needn't reach their ends.
There are 2 independent parts, one for each index of `grp`. The reference program is written for one: setup_inputs(seed, part) draws one part's arguments, and reference() takes and returns one part's arrays. A program takes and returns all parts, laid end to end along the dimension named above; each array names one. Nothing has to cross between parts.
Inputs may be any that keep to these rules, and one draw needn't show every extreme that they name: `vertical_pool`: the 2 entries of one index of ctx are distinct. `vertical_lists`: in row b the first list_counts[b, 0] entries are distinct; later entries are never read. `slash_lists`: row b begins with 0; its first list_counts[b, 1] entries are distinct and none exceeds b or 1 plus b modulo 1; later entries are never read. `list_counts`: column 0 lies between 1 and 6, column 1 between 1 and 2, each reached in every draw.
All inputs are finite; a program needn't handle non-finite values.
Results may differ from the reference program's by a relative error of at most 0.014.
Values may be sent and summed in bfloat16 or wider, within the bound.
A program may use at most 64 MiB of HBM per device.

```python
import jax
import jax.numpy as jnp
from jax import lax

KVH = 8
HD = 128
GROUPS = 8
BLK = 128
P_DEV = 2048
VD = 2
QB_DEV = 1
NQB = 4
QTOT = 512
PREFIX = 8192
POOL = 8
VMAX = 6
SMAX = 2


def draw_queries(key, part):
    drawn = jnp.clip(jax.random.normal(key, (QTOT, KVH, GROUPS, HD), jnp.float32), -8.0, 8.0)
    return drawn.astype(jnp.bfloat16)


def draw_new_keys(key, part):
    drawn = jnp.clip(2.5 * jax.random.normal(key, (QTOT, KVH, HD), jnp.float32), -16.0, 16.0)
    return drawn.astype(jnp.bfloat16)


def draw_vertical_pool(key, part):
    blocks_dev = P_DEV // BLK
    owners = POOL // VD
    subkeys = jax.random.split(jax.random.fold_in(key, 11), owners)
    rows = jax.vmap(lambda subkey: jax.random.permutation(subkey, blocks_dev)[:VD])(subkeys).astype(jnp.int32)
    chosen = jax.random.randint(jax.random.fold_in(key, 12), (), 0, owners)
    position = jnp.arange(VD, dtype=jnp.int32)
    ends = jnp.where(position == VD - 1, blocks_dev - 1, position).astype(jnp.int32)
    rows = jnp.where(jnp.arange(owners)[:, None] == chosen, ends[None, :], rows)
    return rows.reshape(POOL).astype(jnp.int32)


def list_tables(key):
    drawn = jax.random.fold_in(key, 21)
    subkeys = jax.random.split(drawn, 4)
    blocks = jnp.arange(NQB, dtype=jnp.int32)
    jitter = jax.random.randint(subkeys[0], (NQB,), 0, VMAX // 8 + 1)
    jitter = jnp.where(blocks == NQB - 1, 0, jitter)
    vertical_count = jnp.maximum(VMAX * (blocks + 1) // NQB - jitter, 1)
    vertical = jax.vmap(lambda subkey: jax.random.permutation(subkey, POOL)[:VMAX])(jax.random.split(subkeys[1], NQB))
    local_index = blocks % QB_DEV
    reach_limit = jnp.minimum(blocks, QB_DEV + local_index)
    slash_count = jax.random.randint(subkeys[2], (NQB,), 1, reach_limit + 2)
    slash_count = jnp.where(blocks == NQB - 1, reach_limit + 1, slash_count)
    candidates = jax.vmap(lambda subkey: jax.random.permutation(subkey, SMAX - 1) + 1)(jax.random.split(subkeys[3], NQB))
    position = jnp.arange(SMAX - 1, dtype=jnp.int32)
    order_key = (candidates > reach_limit[:, None]).astype(jnp.int32) * SMAX + position[None, :]
    ordering = jnp.argsort(order_key, axis=1)
    ordered = jnp.take_along_axis(candidates, ordering, axis=1)
    slash_rows = jnp.concatenate([jnp.zeros((NQB, 1), jnp.int32), ordered.astype(jnp.int32)], axis=1)
    counts = jnp.stack([vertical_count, slash_count], axis=1)
    return (vertical.astype(jnp.int32), slash_rows.astype(jnp.int32), counts.astype(jnp.int32))


def draw_vertical_lists(key, part):
    return list_tables(key)[0]


def draw_slash_lists(key, part):
    return list_tables(key)[1]


def draw_list_counts(key, part):
    return list_tables(key)[2]


def levels(own_key, extent, pieces, least, high):
    factor_of = 1.0
    for axis_at, parts in pieces:
        heights = jax.random.uniform(jax.random.fold_in(jax.random.fold_in(own_key, 6), axis_at), (parts,), jnp.float32, least / len(pieces), high / len(pieces))
        factor_of = factor_of * jnp.repeat(jnp.exp(heights), extent[axis_at] // parts).reshape((-1,) + (1,) * (len(extent) - 1 - axis_at))
    return factor_of


def bell_draw(rng, dims, width, bound, pieces=(), kind=jnp.bfloat16):
    values = jax.random.normal(rng, dims, jnp.float32) * width
    if len(pieces) > 0:
        values = levels(rng, dims, pieces, -0.22, 0.18) * values
    return jnp.clip(values, min=-bound, max=bound).astype(kind)


def setup_inputs(seed: int = 0, part: int = 0) -> dict:
    arg_keys = jax.random.split(jax.random.key(seed), 10)
    own_keys = jax.random.split(jax.random.fold_in(arg_keys[9], part), 10)
    queries = draw_queries(jax.random.fold_in(jax.random.fold_in(arg_keys[9], part), 71), part)
    new_keys = draw_new_keys(jax.random.fold_in(jax.random.fold_in(arg_keys[9], part), 71), part)
    new_values = bell_draw(own_keys[2], (QTOT, KVH, HD), 1.0, 6.0, ((0, 4), (1, 2)))
    cache_keys = bell_draw(own_keys[3], (PREFIX, KVH, HD), 2.5, 16.0, ((0, 4), (1, 2)))
    cache_values = bell_draw(own_keys[4], (PREFIX, KVH, HD), 1.0, 6.0, ((0, 4), (1, 2)))
    vertical_pool = draw_vertical_pool(jax.random.fold_in(jax.random.fold_in(arg_keys[9], part), 71), part)
    vertical_lists = draw_vertical_lists(jax.random.fold_in(jax.random.fold_in(arg_keys[9], part), 71), part)
    slash_lists = draw_slash_lists(jax.random.fold_in(jax.random.fold_in(arg_keys[9], part), 71), part)
    list_counts = draw_list_counts(jax.random.fold_in(jax.random.fold_in(arg_keys[9], part), 71), part)
    return dict(queries=queries, new_keys=new_keys, new_values=new_values, cache_keys=cache_keys, cache_values=cache_values, vertical_pool=vertical_pool, vertical_lists=vertical_lists, slash_lists=slash_lists, list_counts=list_counts)


def block_update(carry_state, query_block, block_keys, block_values, visible):
    row_peak, row_total, numerator = carry_state
    score_scale = query_block.shape[-1] ** -0.5
    scores = jnp.einsum("rkgd,ckd->rkgc", query_block.astype(jnp.float32), block_keys.astype(jnp.float32)) * score_scale
    scores = jnp.where(visible, scores, -jnp.inf)
    new_peak = jnp.maximum(row_peak, jnp.max(scores, axis=3))
    factor = jnp.exp(row_peak - new_peak)
    weights = jnp.exp(scores - new_peak[..., None])
    row_total = row_total * factor + jnp.sum(weights, axis=3)
    rounded = lax.optimization_barrier(weights.astype(jnp.bfloat16)).astype(jnp.float32)
    numerator = numerator * factor[..., None] + jnp.einsum("rkgc,ckd->rkgd", rounded, block_values.astype(jnp.float32))
    return new_peak, row_total, numerator


def reference(queries, new_keys, new_values, cache_keys, cache_values, vertical_pool, vertical_lists, slash_lists, list_counts):
    blocks_dev = P_DEV // BLK
    owners = jnp.arange(POOL, dtype=jnp.int32) // VD
    pool_sources = (owners * blocks_dev + vertical_pool).astype(jnp.int32)
    cached_keys = cache_keys.reshape(PREFIX // BLK, BLK, KVH, HD)
    cached_values = cache_values.reshape(PREFIX // BLK, BLK, KVH, HD)
    fresh_keys = new_keys.reshape(NQB, BLK, KVH, HD)
    fresh_values = new_values.reshape(NQB, BLK, KVH, HD)
    query_grid = queries.reshape(NQB, BLK, KVH, GROUPS, HD)
    row_ids = lax.broadcasted_iota(jnp.int32, (BLK, 1, 1, BLK), 0)
    col_ids = lax.broadcasted_iota(jnp.int32, (BLK, 1, 1, BLK), 3)
    causal = col_ids <= row_ids

    def one_block(block_index):
        query_block = query_grid[block_index]
        blank_state = (jnp.full((BLK, KVH, GROUPS), -jnp.inf, jnp.float32),
                       jnp.zeros((BLK, KVH, GROUPS), jnp.float32),
                       jnp.zeros((BLK, KVH, GROUPS, HD), jnp.float32))

        def vertical_step(step_index, carry_state):
            source = pool_sources[vertical_lists[block_index, step_index]]
            return block_update(carry_state, query_block, cached_keys[source], cached_values[source], True)

        carry_state = lax.fori_loop(0, list_counts[block_index, 0], vertical_step, blank_state)

        def slash_step(step_index, carry_state):
            offset = slash_lists[block_index, step_index]
            target = block_index - offset
            return block_update(carry_state, query_block, fresh_keys[target], fresh_values[target], causal | (offset > 0))

        carry_state = lax.fori_loop(0, list_counts[block_index, 1], slash_step, carry_state)
        return (carry_state[2] / carry_state[1][..., None]).astype(jnp.bfloat16)

    result = lax.map(one_block, jnp.arange(NQB, dtype=jnp.int32))
    return result.reshape(QTOT, KVH, GROUPS, HD)
```

```python
import functools
import math

import jax
import jax.numpy as jnp
from jax import lax
from jax.experimental import pallas as pl
from jax.experimental.pallas import tpu as pltpu
from jax.sharding import PartitionSpec as P

BLK = 128
MESH = pl.DeviceIdType.MESH


def attend(n, q_ref, own_ref, new_ref, vl_ref, sl_ref, cnt_ref, o_ref,
           pool, slash, acc, peak, total,
           hop_send, hop_recv, sib_send, sib_recv, sl_sem):
    z = lax.axis_index("ctx")
    s = lax.axis_index("sub")
    heads, rows, head_dim = q_ref.shape
    groups = rows // BLK
    c = math.log2(math.e) / math.sqrt(head_dim)
    has_left = z > 0
    has_right = z < n - 1
    sib_id = {"sub": 1 - s}

    barrier = pltpu.get_barrier_semaphore()
    pl.semaphore_signal(barrier, inc=1, device_id=sib_id, device_id_type=MESH)

    @pl.when(has_left)
    def _():
        pl.semaphore_signal(barrier, inc=1, device_id={"ctx": z - 1}, device_id_type=MESH)

    @pl.when(has_right)
    def _():
        pl.semaphore_signal(barrier, inc=1, device_id={"ctx": z + 1}, device_id_type=MESH)

    pl.semaphore_wait(barrier, 1 + has_left.astype(jnp.int32) + has_right.astype(jnp.int32))

    def hop(src_ref, src, kv, right):
        return pltpu.make_async_remote_copy(
            src_ref=src_ref, dst_ref=pool.at[src, s, kv],
            send_sem=hop_send.at[src, int(right), kv], recv_sem=hop_recv.at[src, kv],
            device_id={"ctx": z + 1 if right else z - 1}, device_id_type=MESH)

    def sib(src, kv):
        return pltpu.make_async_remote_copy(
            src_ref=pool.at[src, s, kv], dst_ref=pool.at[src, s, kv],
            send_sem=sib_send.at[src, kv], recv_sem=sib_recv.at[src, kv],
            device_id=sib_id, device_id_type=MESH)

    def sib_in(src, kv):
        return pltpu.make_async_remote_copy(
            src_ref=pool.at[src, 1 - s, kv], dst_ref=pool.at[src, 1 - s, kv],
            send_sem=sib_send.at[src, kv], recv_sem=sib_recv.at[src, kv],
            device_id=sib_id, device_id_type=MESH)

    def slash_hop():
        return pltpu.make_async_remote_copy(
            src_ref=new_ref.at[s], dst_ref=slash.at[s],
            send_sem=sl_sem.at[0], recv_sem=sl_sem.at[1],
            device_id={"ctx": z + 1}, device_id_type=MESH)

    def slash_sib(part):
        return pltpu.make_async_remote_copy(
            src_ref=slash.at[part], dst_ref=slash.at[part],
            send_sem=sl_sem.at[2], recv_sem=sl_sem.at[3],
            device_id=sib_id, device_id_type=MESH)

    @pl.when(has_right)
    def _():
        for kv in range(2):
            hop(own_ref.at[s, kv], z, kv, True).start()

    @pl.when(has_left)
    def _():
        for kv in range(2):
            hop(own_ref.at[s, kv], z, kv, False).start()

    @pl.when((z == 0) & has_right)
    def _():
        slash_hop().start()

    def listed(slot):
        count = cnt_ref[0, 0]
        width = vl_ref.shape[1]
        if width <= 8:
            hit = jnp.int32(0)
            for i in range(width):
                hit = hit | jnp.where((vl_ref[0, i] == slot) & (i < count), 1, 0)
            return hit

        def one(i, hit):
            return hit | jnp.where((vl_ref[0, i] == slot) & (i < count), 1, 0)

        return lax.fori_loop(0, width, one, jnp.int32(0))

    def score(keys, q):
        return lax.dot_general(keys, q, (((1,), (1,)), ((), ())),
                               preferred_element_type=jnp.float32)

    def update(blocks, first=False):
        def one_head(h, carry):
            q = q_ref[h]
            raw = []
            tops = []
            for keys, _, seen in blocks:
                scores = score(keys[h], q)
                if seen is None:
                    key_id = lax.broadcasted_iota(jnp.int32, scores.shape, 0)
                    row_id = lax.broadcasted_iota(jnp.int32, scores.shape, 1) // groups
                    scores = jnp.where(key_id <= row_id, scores, -jnp.inf)
                top = jnp.max(scores, axis=0, keepdims=True)
                if seen is not None:
                    top = jnp.where(seen > 0, top, -jnp.inf)
                raw.append(scores)
                tops.append(top)
            high = functools.reduce(jnp.maximum, tops)
            if not first:
                old = peak[h]
                high = jnp.maximum(old, high)
                factor = jnp.exp2((old - high) * c)
            peak[h] = high
            sums = []
            parts = []
            for (_, values, seen), scores in zip(blocks, raw):
                base = high if seen is None else jnp.where(seen > 0, high, jnp.inf)
                weights = jnp.exp2((scores - base) * c)
                sums.append(jnp.sum(weights, axis=0, keepdims=True))
                parts.append(jnp.dot(values[h], weights.astype(jnp.bfloat16),
                                     preferred_element_type=jnp.float32))
            add_total = sum(sums[1:], sums[0])
            add_acc = sum(parts[1:], parts[0])
            if first:
                total[h] = add_total
                acc[h] = add_acc
            else:
                total[h] = total[h] * factor + add_total
                acc[h] = acc[h] * factor + add_acc
            return carry

        lax.fori_loop(0, heads, one_head, 0)

    update([(new_ref.at[0], new_ref.at[1], None)]
           + [(own_ref.at[b, 0], own_ref.at[b, 1], listed(2 * z + b)) for b in range(2)],
           first=True)

    def pool_update(src):
        update([(pool.at[src, b, 0], pool.at[src, b, 1], listed(2 * src + b))
                for b in range(2)])

    def step(d, carry):
        lo = z - d
        hi = z + d
        for kv in range(2):
            @pl.when(lo >= 0)
            def _():
                hop(own_ref.at[s, kv], lo, kv, True).wait_recv()

                @pl.when(has_right)
                def _():
                    hop(pool.at[lo, s, kv], lo, kv, True).start()

                sib(lo, kv).start()

            @pl.when(hi < n)
            def _():
                hop(own_ref.at[s, kv], hi, kv, False).wait_recv()

                @pl.when(has_left)
                def _():
                    hop(pool.at[hi, s, kv], hi, kv, False).start()

                sib(hi, kv).start()

        @pl.when((d == z) & has_right)
        def _():
            slash_hop().start()

        @pl.when(lo >= 0)
        def _():
            for kv in range(2):
                sib_in(lo, kv).wait_recv()
            pool_update(lo)

        @pl.when(hi < n)
        def _():
            for kv in range(2):
                sib_in(hi, kv).wait_recv()
            pool_update(hi)

        return carry

    lax.fori_loop(1, n, step, 0)

    @pl.when(has_left)
    def _():
        slash_hop().wait_recv()
        slash_sib(s).start()
        slash_sib(1 - s).wait_recv()
        back = jnp.int32(0)
        for i in range(sl_ref.shape[1]):
            back = back | jnp.where((sl_ref[0, i] == 1) & (i < cnt_ref[0, 1]), 1, 0)
        update([(slash.at[0], slash.at[1], back)])
        slash_sib(s).wait_send()

    def finish(h, carry):
        o_ref[h] = jnp.transpose(acc[h] / total[h]).astype(o_ref.dtype)
        return carry

    lax.fori_loop(0, heads, finish, 0)

    def drain(src, carry):
        for kv in range(2):
            @pl.when(has_right & (src <= z))
            def _():
                hop(own_ref.at[s, kv], src, kv, True).wait_send()

            @pl.when(has_left & (src >= z))
            def _():
                hop(own_ref.at[s, kv], src, kv, False).wait_send()

            @pl.when(src != z)
            def _():
                sib(src, kv).wait_send()
        return carry

    lax.fori_loop(0, n, drain, 0)

    @pl.when(has_right)
    def _():
        slash_hop().wait_send()


def shards(n, queries, new_keys, new_values, cache_keys, cache_values,
           vertical_pool, vertical_lists, slash_lists, list_counts):
    tokens, heads, groups, head_dim = queries.shape
    rows = tokens * groups
    picked = vertical_pool.shape[0]

    def pick(cache, order):
        return jnp.stack([
            lax.dynamic_slice_in_dim(cache, vertical_pool[i] * BLK, BLK, 0).transpose(order)
            for i in range(picked)])

    own = jnp.stack([pick(cache_keys, (1, 0, 2)), pick(cache_values, (1, 2, 0))], 1)
    new = jnp.stack([new_keys.transpose(1, 0, 2), new_values.transpose(1, 2, 0)])
    q = queries.transpose(1, 0, 2, 3).reshape(heads, rows, head_dim)
    vmem = pl.BlockSpec(memory_space=pltpu.VMEM)
    smem = pl.BlockSpec(memory_space=pltpu.SMEM)
    dma = pltpu.SemaphoreType.DMA
    out = pl.pallas_call(
        functools.partial(attend, n),
        out_shape=jax.ShapeDtypeStruct((heads, rows, head_dim), jnp.bfloat16),
        in_specs=[vmem, vmem, vmem, smem, smem, smem],
        out_specs=vmem,
        scratch_shapes=[
            pltpu.VMEM((n, picked, 2, heads, BLK, head_dim), jnp.bfloat16),
            pltpu.VMEM((2, heads, BLK, head_dim), jnp.bfloat16),
            pltpu.VMEM((heads, head_dim, rows), jnp.float32),
            pltpu.VMEM((heads, 1, rows), jnp.float32),
            pltpu.VMEM((heads, 1, rows), jnp.float32),
            dma((n, 2, 2)), dma((n, 2)), dma((n, 2)), dma((n, 2)), dma((4,)),
        ],
        compiler_params=pltpu.CompilerParams(
            collective_id=0, has_side_effects=True, vmem_limit_bytes=60 * 2**20),
    )(q, own, new, vertical_lists, slash_lists, list_counts)
    return out.reshape(heads, tokens, groups, head_dim).transpose(1, 0, 2, 3)


def solution(mesh):
    in_specs = (
        P(("grp", "ctx"), "kvh", "sub", None),
        P(("grp", "ctx"), "kvh", None),
        P(("grp", "ctx"), "kvh", None),
        P(("grp", "ctx"), "kvh", None),
        P(("grp", "ctx"), "kvh", None),
        P(("grp", "ctx")),
        P(("grp", "ctx"), None),
        P(("grp", "ctx"), None),
        P(("grp", "ctx"), None),
    )
    out_specs = P(("grp", "ctx"), "kvh", "sub", None)
    return jax.shard_map(functools.partial(shards, mesh.shape["ctx"]), mesh=mesh,
                         in_specs=in_specs, out_specs=out_specs, check_vma=False)
```

```python
import functools
import math

import jax
import jax.numpy as jnp
from jax import lax
from jax.experimental import pallas as pl
from jax.experimental.pallas import tpu as pltpu
from jax.sharding import PartitionSpec as P

BLK = 128
MESH = pl.DeviceIdType.MESH


def attend(n, q_hbm, nk_hbm, nv_hbm, ck_hbm, cv_hbm, vp_ref, vl_ref, sl_ref, cnt_ref, o_ref,
           q_raw, nk_raw, nv_raw, ck_raw, cv_raw, q_ref, own_ref, new_ref, sort_kv, sort_q,
           pool, slash, acc, peak, total,
           hop_send, hop_recv, sib_send, sib_recv, sl_sem, in_sem):
    z = lax.axis_index("ctx")
    s = lax.axis_index("sub")
    heads, rows, head_dim = q_ref.shape
    groups = rows // BLK
    wide = heads * BLK
    loads = [pltpu.make_async_copy(src, dst, in_sem.at[i]) for i, (src, dst) in enumerate(
        [(ck_hbm, ck_raw), (cv_hbm, cv_raw), (nk_hbm, nk_raw), (nv_hbm, nv_raw), (q_hbm, q_raw)])]
    for load in loads:
        load.start()
    c = math.log2(math.e) / math.sqrt(head_dim)
    has_left = z > 0
    has_right = z < n - 1
    sib_id = {"sub": 1 - s}

    barrier = pltpu.get_barrier_semaphore()
    pl.semaphore_signal(barrier, inc=1, device_id=sib_id, device_id_type=MESH)

    @pl.when(has_left)
    def _():
        pl.semaphore_signal(barrier, inc=1, device_id={"ctx": z - 1}, device_id_type=MESH)

    @pl.when(has_right)
    def _():
        pl.semaphore_signal(barrier, inc=1, device_id={"ctx": z + 1}, device_id_type=MESH)

    ids = lax.broadcasted_iota(jnp.int32, (wide, wide), 0)
    at = lax.broadcasted_iota(jnp.int32, (wide, wide), 1)
    sort_kv[...] = jnp.where(at == (ids % BLK) * heads + ids // BLK, 1.0, 0.0).astype(jnp.bfloat16)
    token = (ids % BLK) // groups
    sort_q[...] = jnp.where(at == (token * heads + ids // BLK) * groups + ids % groups,
                            1.0, 0.0).astype(jnp.bfloat16)

    def by_head(raw):
        return jnp.dot(sort_kv[...], raw, preferred_element_type=jnp.float32).astype(jnp.bfloat16)

    def put_keys(dst, raw):
        ordered = by_head(raw)
        for h in range(heads):
            dst[h] = ordered[h * BLK:(h + 1) * BLK]

    def put_values(dst, raw):
        ordered = lax.dot_general(raw, sort_kv[...], (((0,), (1,)), ((), ())),
                                  preferred_element_type=jnp.float32).astype(jnp.bfloat16)
        for h in range(heads):
            dst[h] = ordered[:, h * BLK:(h + 1) * BLK]

    def chosen(cache, b):
        return cache[vp_ref[b]]

    loads[0].wait()
    put_keys(own_ref.at[s, 0], chosen(ck_raw, s))
    loads[1].wait()
    put_values(own_ref.at[s, 1], chosen(cv_raw, s))
    pl.semaphore_wait(barrier, 1 + has_left.astype(jnp.int32) + has_right.astype(jnp.int32))

    def hop(src_ref, src, kv, right):
        return pltpu.make_async_remote_copy(
            src_ref=src_ref, dst_ref=pool.at[src, s, kv],
            send_sem=hop_send.at[src, int(right), kv], recv_sem=hop_recv.at[src, kv],
            device_id={"ctx": z + 1 if right else z - 1}, device_id_type=MESH)

    def sib(src, kv):
        return pltpu.make_async_remote_copy(
            src_ref=pool.at[src, s, kv], dst_ref=pool.at[src, s, kv],
            send_sem=sib_send.at[src, kv], recv_sem=sib_recv.at[src, kv],
            device_id=sib_id, device_id_type=MESH)

    def sib_in(src, kv):
        return pltpu.make_async_remote_copy(
            src_ref=pool.at[src, 1 - s, kv], dst_ref=pool.at[src, 1 - s, kv],
            send_sem=sib_send.at[src, kv], recv_sem=sib_recv.at[src, kv],
            device_id=sib_id, device_id_type=MESH)

    def slash_hop():
        return pltpu.make_async_remote_copy(
            src_ref=new_ref.at[s], dst_ref=slash.at[s],
            send_sem=sl_sem.at[0], recv_sem=sl_sem.at[1],
            device_id={"ctx": z + 1}, device_id_type=MESH)

    def slash_sib(part):
        return pltpu.make_async_remote_copy(
            src_ref=slash.at[part], dst_ref=slash.at[part],
            send_sem=sl_sem.at[2], recv_sem=sl_sem.at[3],
            device_id=sib_id, device_id_type=MESH)

    @pl.when(has_right)
    def _():
        for kv in range(2):
            hop(own_ref.at[s, kv], z, kv, True).start()

    @pl.when(has_left)
    def _():
        for kv in range(2):
            hop(own_ref.at[s, kv], z, kv, False).start()

    loads[2].wait()
    loads[3].wait()
    put_keys(new_ref.at[0], nk_raw[...])
    put_values(new_ref.at[1], nv_raw[...])

    @pl.when((z == 0) & has_right)
    def _():
        slash_hop().start()

    put_keys(own_ref.at[1 - s, 0], chosen(ck_raw, 1 - s))
    put_values(own_ref.at[1 - s, 1], chosen(cv_raw, 1 - s))
    loads[4].wait()
    for part in range(rows // BLK):
        ordered = jnp.dot(sort_q[...], q_raw[part * wide:(part + 1) * wide],
                          preferred_element_type=jnp.float32).astype(jnp.bfloat16)
        for h in range(heads):
            q_ref[h, part * BLK:(part + 1) * BLK] = ordered[h * BLK:(h + 1) * BLK]

    def listed(slot):
        count = cnt_ref[0, 0]
        width = vl_ref.shape[1]
        if width <= 8:
            hit = jnp.int32(0)
            for i in range(width):
                hit = hit | jnp.where((vl_ref[0, i] == slot) & (i < count), 1, 0)
            return hit

        def one(i, hit):
            return hit | jnp.where((vl_ref[0, i] == slot) & (i < count), 1, 0)

        return lax.fori_loop(0, width, one, jnp.int32(0))

    def score(keys, q):
        return lax.dot_general(keys, q, (((1,), (1,)), ((), ())),
                               preferred_element_type=jnp.float32)

    def update(blocks, first=False):
        def one_head(h):
            q = q_ref[h]
            raw = []
            tops = []
            for keys, _, seen in blocks:
                scores = score(keys[h], q)
                if seen is None:
                    key_id = lax.broadcasted_iota(jnp.int32, scores.shape, 0)
                    row_id = lax.broadcasted_iota(jnp.int32, scores.shape, 1) // groups
                    scores = jnp.where(key_id <= row_id, scores, -jnp.inf)
                top = jnp.max(scores, axis=0, keepdims=True)
                if seen is not None:
                    top = jnp.where(seen > 0, top, -jnp.inf)
                raw.append(scores)
                tops.append(top)
            high = functools.reduce(jnp.maximum, tops)
            if not first:
                old = peak[h]
                high = jnp.maximum(old, high)
                factor = jnp.exp2((old - high) * c)
            peak[h] = high
            sums = []
            parts = []
            for (_, values, seen), scores in zip(blocks, raw):
                base = high if seen is None else jnp.where(seen > 0, high, jnp.inf)
                weights = jnp.exp2((scores - base) * c)
                sums.append(jnp.sum(weights, axis=0, keepdims=True))
                parts.append(jnp.dot(values[h], weights.astype(jnp.bfloat16),
                                     preferred_element_type=jnp.float32))
            add_total = sum(sums[1:], sums[0])
            add_acc = sum(parts[1:], parts[0])
            if first:
                total[h] = add_total
                acc[h] = add_acc
            else:
                total[h] = total[h] * factor + add_total
                acc[h] = acc[h] * factor + add_acc

        for h in range(heads):
            one_head(h)

    update([(new_ref.at[0], new_ref.at[1], None)]
           + [(own_ref.at[b, 0], own_ref.at[b, 1], listed(2 * z + b)) for b in range(2)],
           first=True)

    def pool_update(src):
        update([(pool.at[src, b, 0], pool.at[src, b, 1], listed(2 * src + b))
                for b in range(2)])

    def step(d, carry):
        lo = z - d
        hi = z + d
        for kv in range(2):
            @pl.when(lo >= 0)
            def _():
                hop(own_ref.at[s, kv], lo, kv, True).wait_recv()

                @pl.when(has_right)
                def _():
                    hop(pool.at[lo, s, kv], lo, kv, True).start()

                sib(lo, kv).start()

            @pl.when(hi < n)
            def _():
                hop(own_ref.at[s, kv], hi, kv, False).wait_recv()

                @pl.when(has_left)
                def _():
                    hop(pool.at[hi, s, kv], hi, kv, False).start()

                sib(hi, kv).start()

        @pl.when((d == z) & has_right)
        def _():
            slash_hop().start()

        @pl.when(lo >= 0)
        def _():
            for kv in range(2):
                sib_in(lo, kv).wait_recv()
            pool_update(lo)

        @pl.when(hi < n)
        def _():
            for kv in range(2):
                sib_in(hi, kv).wait_recv()
            pool_update(hi)

        return carry

    lax.fori_loop(1, n, step, 0)

    @pl.when(has_left)
    def _():
        slash_hop().wait_recv()
        slash_sib(s).start()
        slash_sib(1 - s).wait_recv()
        back = jnp.int32(0)
        for i in range(sl_ref.shape[1]):
            back = back | jnp.where((sl_ref[0, i] == 1) & (i < cnt_ref[0, 1]), 1, 0)
        update([(slash.at[0], slash.at[1], back)])
        slash_sib(s).wait_send()

    for part in range(rows // BLK):
        lanes = slice(part * BLK, (part + 1) * BLK)
        done = jnp.concatenate(
            [(acc[h, :, lanes] / total[h, :, lanes]).astype(jnp.bfloat16) for h in range(heads)], 1)
        o_ref[part * wide:(part + 1) * wide] = lax.dot_general(
            sort_q[...], done, (((0,), (1,)), ((), ())),
            preferred_element_type=jnp.float32).astype(o_ref.dtype)

    def drain(src, carry):
        for kv in range(2):
            @pl.when(has_right & (src <= z))
            def _():
                hop(own_ref.at[s, kv], src, kv, True).wait_send()

            @pl.when(has_left & (src >= z))
            def _():
                hop(own_ref.at[s, kv], src, kv, False).wait_send()

            @pl.when(src != z)
            def _():
                sib(src, kv).wait_send()
        return carry

    lax.fori_loop(0, n, drain, 0)

    @pl.when(has_right)
    def _():
        slash_hop().wait_send()


def shards(n, queries, new_keys, new_values, cache_keys, cache_values,
           vertical_pool, vertical_lists, slash_lists, list_counts):
    tokens, heads, groups, head_dim = queries.shape
    rows = tokens * groups
    picked = vertical_pool.shape[0]

    def flat(x):
        return x.reshape(-1, head_dim)

    def vmem(*shape):
        return pltpu.VMEM(shape, jnp.bfloat16)

    hbm = pl.BlockSpec(memory_space=pl.ANY)
    smem = pl.BlockSpec(memory_space=pltpu.SMEM)
    dma = pltpu.SemaphoreType.DMA
    wide = heads * BLK
    cached = cache_keys.shape[0] // BLK
    out = pl.pallas_call(
        functools.partial(attend, n),
        out_shape=jax.ShapeDtypeStruct((tokens * heads * groups, head_dim), jnp.bfloat16),
        in_specs=[hbm] * 5 + [smem] * 4,
        out_specs=pl.BlockSpec(memory_space=pltpu.VMEM),
        scratch_shapes=[
            vmem(heads * rows, head_dim), vmem(wide, head_dim), vmem(wide, head_dim),
            vmem(cached, wide, head_dim), vmem(cached, wide, head_dim),
            vmem(heads, rows, head_dim), vmem(picked, 2, heads, BLK, head_dim),
            vmem(2, heads, BLK, head_dim), vmem(wide, wide), vmem(wide, wide),
            vmem(n, picked, 2, heads, BLK, head_dim),
            vmem(2, heads, BLK, head_dim),
            pltpu.VMEM((heads, head_dim, rows), jnp.float32),
            pltpu.VMEM((heads, 1, rows), jnp.float32),
            pltpu.VMEM((heads, 1, rows), jnp.float32),
            dma((n, 2, 2)), dma((n, 2)), dma((n, 2)), dma((n, 2)), dma((4,)), dma((5,)),
        ],
        compiler_params=pltpu.CompilerParams(
            collective_id=0, has_side_effects=True, vmem_limit_bytes=60 * 2**20),
    )(flat(queries), flat(new_keys), flat(new_values), cache_keys.reshape(cached, wide, head_dim),
      cache_values.reshape(cached, wide, head_dim),
      vertical_pool, vertical_lists, slash_lists, list_counts)
    return out.reshape(tokens, heads, groups, head_dim)


def solution(mesh):
    in_specs = (
        P(("grp", "ctx"), "kvh", "sub", None),
        P(("grp", "ctx"), "kvh", None),
        P(("grp", "ctx"), "kvh", None),
        P(("grp", "ctx"), "kvh", None),
        P(("grp", "ctx"), "kvh", None),
        P(("grp", "ctx")),
        P(("grp", "ctx"), None),
        P(("grp", "ctx"), None),
        P(("grp", "ctx"), None),
    )
    out_specs = P(("grp", "ctx"), "kvh", "sub", None)
    return jax.shard_map(functools.partial(shards, mesh.shape["ctx"]), mesh=mesh,
                         in_specs=in_specs, out_specs=out_specs, check_vma=False)
```

```python
import functools
import math

import jax
import jax.numpy as jnp
from jax import lax
from jax.experimental import pallas as pl
from jax.experimental.pallas import tpu as pltpu
from jax.sharding import PartitionSpec as P

BLK = 128
MESH = pl.DeviceIdType.MESH


def attend(n, q_hbm, nk_hbm, nv_hbm, ck_hbm, cv_hbm, vp_ref, vl_ref, sl_ref, cnt_ref, o_ref,
           q_raw, nk_raw, nv_raw, ck_raw, cv_raw, q_ref, own_ref, new_ref, sort_kv, sort_q,
           pool, slash_raw, slash, acc, peak, total, rounded, fade,
           hop_send, hop_recv, sib_send, sib_recv, sl_sem, in_sem):
    z = lax.axis_index("ctx")
    s = lax.axis_index("sub")
    heads, rows, head_dim = q_ref.shape
    groups = rows // BLK
    wide = heads * BLK
    loads = [pltpu.make_async_copy(src, dst, in_sem.at[i]) for i, (src, dst) in enumerate(
        [(ck_hbm, ck_raw), (cv_hbm, cv_raw), (nk_hbm, nk_raw), (nv_hbm, nv_raw), (q_hbm, q_raw)])]
    loads[0].start()
    loads[1].start()
    c = math.log2(math.e) / math.sqrt(head_dim)
    has_left = z > 0
    has_right = z < n - 1
    sib_id = {"sub": 1 - s}

    barrier = pltpu.get_barrier_semaphore()
    pl.semaphore_signal(barrier, inc=1, device_id=sib_id, device_id_type=MESH)

    @pl.when(has_left)
    def _():
        pl.semaphore_signal(barrier, inc=1, device_id={"ctx": z - 1}, device_id_type=MESH)

    @pl.when(has_right)
    def _():
        pl.semaphore_signal(barrier, inc=1, device_id={"ctx": z + 1}, device_id_type=MESH)

    ids = lax.broadcasted_iota(jnp.int32, (wide, wide), 0)
    at = lax.broadcasted_iota(jnp.int32, (wide, wide), 1)
    sort_kv[...] = jnp.where(at == (ids % BLK) * heads + ids // BLK, 1.0, 0.0).astype(jnp.bfloat16)
    token = (ids % BLK) // groups
    sort_q[...] = jnp.where(at == (token * heads + ids // BLK) * groups + ids % groups,
                            1.0, 0.0).astype(jnp.bfloat16)

    def by_head(raw):
        return jnp.dot(sort_kv[...], raw, preferred_element_type=jnp.float32).astype(jnp.bfloat16)

    def put_keys(dst, raw):
        ordered = by_head(raw)
        for h in range(heads):
            dst[h] = ordered[h * BLK:(h + 1) * BLK]

    def put_values(dst, raw):
        ordered = lax.dot_general(raw, sort_kv[...], (((0,), (1,)), ((), ())),
                                  preferred_element_type=jnp.float32).astype(jnp.bfloat16)
        for h in range(heads):
            dst[h] = ordered[:, h * BLK:(h + 1) * BLK]

    def chosen(cache, b):
        return cache[vp_ref[b]]

    pl.semaphore_wait(barrier, 1 + has_left.astype(jnp.int32) + has_right.astype(jnp.int32))

    def hop(src_ref, src, kv, right):
        return pltpu.make_async_remote_copy(
            src_ref=src_ref, dst_ref=pool.at[src, s, kv],
            send_sem=hop_send.at[src, int(right), kv], recv_sem=hop_recv.at[src, kv],
            device_id={"ctx": z + 1 if right else z - 1}, device_id_type=MESH)

    def sib(src, kv):
        return pltpu.make_async_remote_copy(
            src_ref=pool.at[src, s, kv], dst_ref=pool.at[src, s, kv],
            send_sem=sib_send.at[src, kv], recv_sem=sib_recv.at[src, kv],
            device_id=sib_id, device_id_type=MESH)

    def sib_in(src, kv):
        return pltpu.make_async_remote_copy(
            src_ref=pool.at[src, 1 - s, kv], dst_ref=pool.at[src, 1 - s, kv],
            send_sem=sib_send.at[src, kv], recv_sem=sib_recv.at[src, kv],
            device_id=sib_id, device_id_type=MESH)

    def slash_hop(src_ref=nk_hbm):
        return pltpu.make_async_remote_copy(
            src_ref=src_ref, dst_ref=slash_raw.at[s],
            send_sem=sl_sem.at[0], recv_sem=sl_sem.at[1],
            device_id={"ctx": z + 1}, device_id_type=MESH)

    def slash_sib(part):
        return pltpu.make_async_remote_copy(
            src_ref=slash_raw.at[part], dst_ref=slash_raw.at[part],
            send_sem=sl_sem.at[2], recv_sem=sl_sem.at[3],
            device_id=sib_id, device_id_type=MESH)

    for part, src_ref in enumerate((nk_hbm, nv_hbm)):
        @pl.when(has_right & (s == part))
        def _():
            slash_hop(src_ref).start()

    def send_own(kv):
        @pl.when(has_right)
        def _():
            hop(own_ref.at[s, kv], z, kv, True).start()

        @pl.when(has_left)
        def _():
            hop(own_ref.at[s, kv], z, kv, False).start()

    loads[0].wait()
    put_keys(own_ref.at[s, 0], chosen(ck_raw, s))
    for load in loads[2:]:
        load.start()
    send_own(0)
    loads[1].wait()
    put_values(own_ref.at[s, 1], chosen(cv_raw, s))
    send_own(1)
    loads[2].wait()
    loads[3].wait()
    put_keys(new_ref.at[0], nk_raw[...])
    put_values(new_ref.at[1], nv_raw[...])
    put_keys(own_ref.at[1 - s, 0], chosen(ck_raw, 1 - s))
    put_values(own_ref.at[1 - s, 1], chosen(cv_raw, 1 - s))
    loads[4].wait()
    for part in range(rows // BLK):
        ordered = jnp.dot(sort_q[...], q_raw[part * wide:(part + 1) * wide],
                          preferred_element_type=jnp.float32).astype(jnp.bfloat16)
        for h in range(heads):
            q_ref[h, part * BLK:(part + 1) * BLK] = ordered[h * BLK:(h + 1) * BLK]

    def listed(slot):
        count = cnt_ref[0, 0]
        width = vl_ref.shape[1]
        if width <= 8:
            hit = jnp.int32(0)
            for i in range(width):
                hit = hit | jnp.where((vl_ref[0, i] == slot) & (i < count), 1, 0)
            return hit

        def one(i, hit):
            return hit | jnp.where((vl_ref[0, i] == slot) & (i < count), 1, 0)

        return lax.fori_loop(0, width, one, jnp.int32(0))

    def score(keys, q):
        return lax.dot_general(keys, q, (((1,), (1,)), ((), ())),
                               preferred_element_type=jnp.float32)

    def take_keys(side, blocks, first=False):
        for h in range(heads):
            q = q_ref[h]
            raw = []
            tops = []
            for keys, seen in blocks:
                scores = score(keys[h], q)
                if seen is None:
                    key_id = lax.broadcasted_iota(jnp.int32, scores.shape, 0)
                    row_id = lax.broadcasted_iota(jnp.int32, scores.shape, 1) // groups
                    scores = jnp.where(key_id <= row_id, scores, -jnp.inf)
                top = jnp.max(scores, axis=0, keepdims=True)
                if seen is not None:
                    top = jnp.where(seen > 0, top, -jnp.inf)
                raw.append(scores)
                tops.append(top)
            high = functools.reduce(jnp.maximum, tops)
            if not first:
                old = peak[h]
                high = jnp.maximum(old, high)
                factor = jnp.exp2((old - high) * c)
                fade[side, h] = factor
            peak[h] = high
            sums = []
            for i, ((_, seen), scores) in enumerate(zip(blocks, raw)):
                base = high if seen is None else jnp.where(seen > 0, high, jnp.inf)
                weights = jnp.exp2((scores - base) * c)
                sums.append(jnp.sum(weights, axis=0, keepdims=True))
                rounded[side, h, i * BLK:(i + 1) * BLK] = weights.astype(jnp.bfloat16)
            add = sum(sums[1:], sums[0])
            total[h] = add if first else total[h] * fade[side, h] + add

    def take_values(side, blocks, first=False):
        depth = len(blocks) * BLK
        for h in range(heads):
            values = jnp.concatenate([values[h] for values in blocks], 1)
            add = jnp.dot(values, rounded[side, h, :depth], preferred_element_type=jnp.float32)
            acc[h] = add if first else acc[h] * fade[side, h] + add

    take_keys(0, [(new_ref.at[0], None)]
              + [(own_ref.at[b, 0], listed(2 * z + b)) for b in range(2)], first=True)
    take_values(0, [new_ref.at[1]] + [own_ref.at[b, 1] for b in range(2)], first=True)

    @pl.when(has_left)
    def _():
        slash_hop().wait_recv()
        slash_sib(s).start()

    def arrive(src, kv, right):
        hop(own_ref.at[s, kv], src, kv, right).wait_recv()

        @pl.when(has_right if right else has_left)
        def _():
            hop(pool.at[src, s, kv], src, kv, right).start()

        sib(src, kv).start()

    def step(d, carry):
        sides = ((z - d, z - d >= 0, True), (z + d, z + d < n, False))
        for kv in range(2):
            for src, there, right in sides:
                @pl.when(there)
                def _():
                    arrive(src, kv, right)

            if kv == 0:
                @pl.when((d == 1) & has_left)
                def _():
                    slash_sib(1 - s).wait_recv()
                    put_keys(slash.at[0], slash_raw[0])
                    put_values(slash.at[1], slash_raw[1])
                    back = jnp.int32(0)
                    for i in range(sl_ref.shape[1]):
                        back = back | jnp.where((sl_ref[0, i] == 1) & (i < cnt_ref[0, 1]), 1, 0)
                    take_keys(0, [(slash.at[0], back)])
                    take_values(0, [slash.at[1]])

            for side, (src, there, right) in enumerate(sides):
                @pl.when(there)
                def _():
                    sib_in(src, kv).wait_recv()
                    if kv == 0:
                        take_keys(side, [(pool.at[src, b, 0], listed(2 * src + b))
                                         for b in range(2)])
                    else:
                        take_values(side, [pool.at[src, b, 1] for b in range(2)])

        return carry

    lax.fori_loop(1, n, step, 0)

    for part in range(rows // BLK):
        lanes = slice(part * BLK, (part + 1) * BLK)
        done = jnp.concatenate(
            [(acc[h, :, lanes] / total[h, :, lanes]).astype(jnp.bfloat16) for h in range(heads)], 1)
        o_ref[part * wide:(part + 1) * wide] = lax.dot_general(
            sort_q[...], done, (((0,), (1,)), ((), ())),
            preferred_element_type=jnp.float32).astype(o_ref.dtype)

    def drain(src, carry):
        for kv in range(2):
            @pl.when(has_right & (src <= z))
            def _():
                hop(own_ref.at[s, kv], src, kv, True).wait_send()

            @pl.when(has_left & (src >= z))
            def _():
                hop(own_ref.at[s, kv], src, kv, False).wait_send()

            @pl.when(src != z)
            def _():
                sib(src, kv).wait_send()
        return carry

    lax.fori_loop(0, n, drain, 0)

    @pl.when(has_right)
    def _():
        slash_hop().wait_send()

    @pl.when(has_left)
    def _():
        slash_sib(s).wait_send()


def shards(n, queries, new_keys, new_values, cache_keys, cache_values,
           vertical_pool, vertical_lists, slash_lists, list_counts):
    tokens, heads, groups, head_dim = queries.shape
    rows = tokens * groups
    picked = vertical_pool.shape[0]

    def flat(x):
        return x.reshape(-1, head_dim)

    def vmem(*shape):
        return pltpu.VMEM(shape, jnp.bfloat16)

    hbm = pl.BlockSpec(memory_space=pl.ANY)
    smem = pl.BlockSpec(memory_space=pltpu.SMEM)
    dma = pltpu.SemaphoreType.DMA
    wide = heads * BLK
    cached = cache_keys.shape[0] // BLK
    out = pl.pallas_call(
        functools.partial(attend, n),
        out_shape=jax.ShapeDtypeStruct((tokens * heads * groups, head_dim), jnp.bfloat16),
        in_specs=[hbm] * 5 + [smem] * 4,
        out_specs=pl.BlockSpec(memory_space=pltpu.VMEM),
        scratch_shapes=[
            vmem(heads * rows, head_dim), vmem(wide, head_dim), vmem(wide, head_dim),
            vmem(cached, wide, head_dim), vmem(cached, wide, head_dim),
            vmem(heads, rows, head_dim), vmem(picked, 2, heads, BLK, head_dim),
            vmem(2, heads, BLK, head_dim), vmem(wide, wide), vmem(wide, wide),
            vmem(n, picked, 2, heads, BLK, head_dim),
            vmem(2, wide, head_dim), vmem(2, heads, BLK, head_dim),
            pltpu.VMEM((heads, head_dim, rows), jnp.float32),
            pltpu.VMEM((heads, 1, rows), jnp.float32),
            pltpu.VMEM((heads, 1, rows), jnp.float32),
            vmem(2, heads, 3 * BLK, rows), pltpu.VMEM((2, heads, 1, rows), jnp.float32),
            dma((n, 2, 2)), dma((n, 2)), dma((n, 2)), dma((n, 2)), dma((4,)), dma((5,)),
        ],
        compiler_params=pltpu.CompilerParams(
            collective_id=0, has_side_effects=True, vmem_limit_bytes=60 * 2**20),
    )(flat(queries), flat(new_keys), flat(new_values), cache_keys.reshape(cached, wide, head_dim),
      cache_values.reshape(cached, wide, head_dim),
      vertical_pool, vertical_lists, slash_lists, list_counts)
    return out.reshape(tokens, heads, groups, head_dim)


def solution(mesh):
    in_specs = (
        P(("grp", "ctx"), "kvh", "sub", None),
        P(("grp", "ctx"), "kvh", None),
        P(("grp", "ctx"), "kvh", None),
        P(("grp", "ctx"), "kvh", None),
        P(("grp", "ctx"), "kvh", None),
        P(("grp", "ctx")),
        P(("grp", "ctx"), None),
        P(("grp", "ctx"), None),
        P(("grp", "ctx"), None),
    )
    out_specs = P(("grp", "ctx"), "kvh", "sub", None)
    return jax.shard_map(functools.partial(shards, mesh.shape["ctx"]), mesh=mesh,
                         in_specs=in_specs, out_specs=out_specs, check_vma=False)
```

```python
import functools
import math

import jax
import jax.numpy as jnp
from jax import lax
from jax.experimental import pallas as pl
from jax.experimental.pallas import tpu as pltpu
from jax.sharding import PartitionSpec as P

BLK = 128
MESH = pl.DeviceIdType.MESH


def attend(n, q_hbm, nk_hbm, nv_hbm, ck_hbm, cv_hbm, vp_ref, vl_ref, sl_ref, cnt_ref, o_ref,
           q_raw, nk_raw, nv_raw, ck_raw, cv_raw, q_ref, own_ref, new_ref, sort_kv, sort_q,
           pool, slash_raw, slash, acc, peak, total, rounded, fade,
           hop_send, hop_recv, sib_send, sib_recv, sl_sem, in_sem):
    z = lax.axis_index("ctx")
    s = lax.axis_index("sub")
    heads, rows, head_dim = q_ref.shape
    groups = rows // BLK
    wide = heads * BLK
    loads = [pltpu.make_async_copy(src, dst, in_sem.at[i]) for i, (src, dst) in enumerate(
        [(ck_hbm, ck_raw), (cv_hbm, cv_raw), (nk_hbm, nk_raw), (nv_hbm, nv_raw), (q_hbm, q_raw)])]
    loads[0].start()
    c = math.log2(math.e) / math.sqrt(head_dim)
    has_left = z > 0
    has_right = z < n - 1
    sib_id = {"sub": 1 - s}

    barrier = pltpu.get_barrier_semaphore()
    pl.semaphore_signal(barrier, inc=1, device_id=sib_id, device_id_type=MESH)

    @pl.when(has_left)
    def _():
        pl.semaphore_signal(barrier, inc=1, device_id={"ctx": z - 1}, device_id_type=MESH)

    @pl.when(has_right)
    def _():
        pl.semaphore_signal(barrier, inc=1, device_id={"ctx": z + 1}, device_id_type=MESH)

    ids = lax.broadcasted_iota(jnp.int32, (wide, wide), 0)
    at = lax.broadcasted_iota(jnp.int32, (wide, wide), 1)
    sort_kv[...] = jnp.where(at == (ids % BLK) * heads + ids // BLK, 1.0, 0.0).astype(jnp.bfloat16)
    token = (ids % BLK) // groups
    sort_q[...] = jnp.where(at == (token * heads + ids // BLK) * groups + ids % groups,
                            1.0, 0.0).astype(jnp.bfloat16)

    def by_head(raw):
        return jnp.dot(sort_kv[...], raw, preferred_element_type=jnp.float32).astype(jnp.bfloat16)

    def put_keys(dst, raw):
        ordered = by_head(raw)
        for h in range(heads):
            dst[h] = ordered[h * BLK:(h + 1) * BLK]

    def put_values(dst, raw):
        ordered = lax.dot_general(raw, sort_kv[...], (((0,), (1,)), ((), ())),
                                  preferred_element_type=jnp.float32).astype(jnp.bfloat16)
        for h in range(heads):
            dst[h] = ordered[:, h * BLK:(h + 1) * BLK]

    def chosen(cache, b):
        return cache[vp_ref[b]]

    pl.semaphore_wait(barrier, 1 + has_left.astype(jnp.int32) + has_right.astype(jnp.int32))

    def hop(src_ref, src, kv, right):
        return pltpu.make_async_remote_copy(
            src_ref=src_ref, dst_ref=pool.at[src, s, kv],
            send_sem=hop_send.at[src, int(right), kv], recv_sem=hop_recv.at[src, kv],
            device_id={"ctx": z + 1 if right else z - 1}, device_id_type=MESH)

    def sib(src, kv):
        return pltpu.make_async_remote_copy(
            src_ref=pool.at[src, s, kv], dst_ref=pool.at[src, s, kv],
            send_sem=sib_send.at[src, kv], recv_sem=sib_recv.at[src, kv],
            device_id=sib_id, device_id_type=MESH)

    def sib_in(src, kv):
        return pltpu.make_async_remote_copy(
            src_ref=pool.at[src, 1 - s, kv], dst_ref=pool.at[src, 1 - s, kv],
            send_sem=sib_send.at[src, kv], recv_sem=sib_recv.at[src, kv],
            device_id=sib_id, device_id_type=MESH)

    def slash_hop(src_ref=nk_hbm):
        return pltpu.make_async_remote_copy(
            src_ref=src_ref, dst_ref=slash_raw.at[s],
            send_sem=sl_sem.at[0], recv_sem=sl_sem.at[1],
            device_id={"ctx": z + 1}, device_id_type=MESH)

    def slash_sib(part):
        return pltpu.make_async_remote_copy(
            src_ref=slash_raw.at[part], dst_ref=slash_raw.at[part],
            send_sem=sl_sem.at[2], recv_sem=sl_sem.at[3],
            device_id=sib_id, device_id_type=MESH)

    for part, src_ref in enumerate((nk_hbm, nv_hbm)):
        @pl.when(has_right & (s == part))
        def _():
            slash_hop(src_ref).start()

    def send_own(kv):
        @pl.when(has_right)
        def _():
            hop(own_ref.at[s, kv], z, kv, True).start()

        @pl.when(has_left)
        def _():
            hop(own_ref.at[s, kv], z, kv, False).start()

    loads[0].wait()
    loads[1].start()
    put_keys(own_ref.at[s, 0], chosen(ck_raw, s))
    for load in loads[2:]:
        load.start()
    send_own(0)
    loads[1].wait()
    put_values(own_ref.at[s, 1], chosen(cv_raw, s))
    send_own(1)
    loads[2].wait()
    loads[3].wait()
    put_keys(new_ref.at[0], nk_raw[...])
    put_values(new_ref.at[1], nv_raw[...])
    put_keys(own_ref.at[1 - s, 0], chosen(ck_raw, 1 - s))
    put_values(own_ref.at[1 - s, 1], chosen(cv_raw, 1 - s))
    loads[4].wait()
    for part in range(rows // BLK):
        ordered = jnp.dot(sort_q[...], q_raw[part * wide:(part + 1) * wide],
                          preferred_element_type=jnp.float32).astype(jnp.bfloat16)
        for h in range(heads):
            q_ref[h, part * BLK:(part + 1) * BLK] = ordered[h * BLK:(h + 1) * BLK]

    def listed(slot):
        count = cnt_ref[0, 0]
        width = vl_ref.shape[1]
        if width <= 8:
            hit = jnp.int32(0)
            for i in range(width):
                hit = hit | jnp.where((vl_ref[0, i] == slot) & (i < count), 1, 0)
            return hit

        def one(i, hit):
            return hit | jnp.where((vl_ref[0, i] == slot) & (i < count), 1, 0)

        return lax.fori_loop(0, width, one, jnp.int32(0))

    def score(keys, q):
        return lax.dot_general(keys, q, (((1,), (1,)), ((), ())),
                               preferred_element_type=jnp.float32)

    def take_keys(side, blocks, first=False):
        for h in range(heads):
            q = q_ref[h]
            raw = []
            tops = []
            for keys, seen in blocks:
                scores = score(keys[h], q)
                if seen is None:
                    key_id = lax.broadcasted_iota(jnp.int32, scores.shape, 0)
                    row_id = lax.broadcasted_iota(jnp.int32, scores.shape, 1) // groups
                    scores = jnp.where(key_id <= row_id, scores, -jnp.inf)
                top = jnp.max(scores, axis=0, keepdims=True)
                if seen is not None:
                    top = jnp.where(seen > 0, top, -jnp.inf)
                raw.append(scores)
                tops.append(top)
            high = functools.reduce(jnp.maximum, tops)
            if not first:
                old = peak[h]
                high = jnp.maximum(old, high)
                factor = jnp.exp2((old - high) * c)
                fade[side, h] = factor
            peak[h] = high
            sums = []
            for i, ((_, seen), scores) in enumerate(zip(blocks, raw)):
                base = high if seen is None else jnp.where(seen > 0, high, jnp.inf)
                weights = jnp.exp2((scores - base) * c)
                sums.append(jnp.sum(weights, axis=0, keepdims=True))
                rounded[side, h, i * BLK:(i + 1) * BLK] = weights.astype(jnp.bfloat16)
            add = sum(sums[1:], sums[0])
            total[h] = add if first else total[h] * fade[side, h] + add

    def take_values(side, blocks, first=False):
        depth = len(blocks) * BLK
        for h in range(heads):
            values = jnp.concatenate([values[h] for values in blocks], 1)
            add = jnp.dot(values, rounded[side, h, :depth], preferred_element_type=jnp.float32)
            acc[h] = add if first else acc[h] * fade[side, h] + add

    take_keys(0, [(new_ref.at[0], None)]
              + [(own_ref.at[b, 0], listed(2 * z + b)) for b in range(2)], first=True)
    take_values(0, [new_ref.at[1]] + [own_ref.at[b, 1] for b in range(2)], first=True)

    @pl.when(has_left)
    def _():
        slash_hop().wait_recv()
        slash_sib(s).start()

    def arrive(src, kv, right):
        hop(own_ref.at[s, kv], src, kv, right).wait_recv()

        @pl.when(has_right if right else has_left)
        def _():
            hop(pool.at[src, s, kv], src, kv, right).start()

        sib(src, kv).start()

    def step(d, carry):
        sides = ((z + d, z + d < n, False), (z - d, z - d >= 0, True))
        for kv in range(2):
            for src, there, right in sides:
                @pl.when(there)
                def _():
                    arrive(src, kv, right)

            for side, (src, there, right) in enumerate(sides):
                @pl.when(there)
                def _():
                    sib_in(src, kv).wait_recv()
                    if kv == 0:
                        take_keys(side, [(pool.at[src, b, 0], listed(2 * src + b))
                                         for b in range(2)])
                    else:
                        take_values(side, [pool.at[src, b, 1] for b in range(2)])

        @pl.when((d == 1) & has_left)
        def _():
            slash_sib(1 - s).wait_recv()
            put_keys(slash.at[0], slash_raw[0])
            put_values(slash.at[1], slash_raw[1])
            back = jnp.int32(0)
            for i in range(sl_ref.shape[1]):
                back = back | jnp.where((sl_ref[0, i] == 1) & (i < cnt_ref[0, 1]), 1, 0)
            take_keys(0, [(slash.at[0], back)])
            take_values(0, [slash.at[1]])

        return carry

    lax.fori_loop(1, n, step, 0)

    for h in range(heads):
        done = (acc[h] / total[h]).astype(jnp.bfloat16)
        for part in range(rows // BLK):
            o_ref[part, :, h * BLK:(h + 1) * BLK] = done[:, part * BLK:(part + 1) * BLK]

    def drain(src, carry):
        for kv in range(2):
            @pl.when(has_right & (src <= z))
            def _():
                hop(own_ref.at[s, kv], src, kv, True).wait_send()

            @pl.when(has_left & (src >= z))
            def _():
                hop(own_ref.at[s, kv], src, kv, False).wait_send()

            @pl.when(src != z)
            def _():
                sib(src, kv).wait_send()
        return carry

    lax.fori_loop(0, n, drain, 0)

    @pl.when(has_right)
    def _():
        slash_hop().wait_send()

    @pl.when(has_left)
    def _():
        slash_sib(s).wait_send()


def restore(heads, groups, x_hbm, o_hbm, x_ref, staged, in_sem, sem):
    parts, _, wide = x_ref.shape
    loads = [pltpu.make_async_copy(x_hbm.at[part], x_ref.at[part], in_sem.at[part])
             for part in range(parts)]
    for load in loads:
        load.start()
    ids = lax.broadcasted_iota(jnp.int32, (wide, wide), 1)
    at = lax.broadcasted_iota(jnp.int32, (wide, wide), 0)
    token = (ids % BLK) // groups
    unsort = jnp.where(at == (token * heads + ids // BLK) * groups + ids % groups,
                       1.0, 0.0).astype(jnp.bfloat16)
    copies = []
    for part in range(parts):
        loads[part].wait()
        staged[part] = lax.dot_general(
            unsort, x_ref[part], (((1,), (1,)), ((), ())),
            preferred_element_type=jnp.float32).astype(jnp.bfloat16)
        copy = pltpu.make_async_copy(
            staged.at[part], o_hbm.at[pl.ds(part * wide, wide)], sem.at[part])
        copy.start()
        copies.append(copy)
    for copy in copies:
        copy.wait()


def shards(n, queries, new_keys, new_values, cache_keys, cache_values,
           vertical_pool, vertical_lists, slash_lists, list_counts):
    tokens, heads, groups, head_dim = queries.shape
    rows = tokens * groups
    picked = vertical_pool.shape[0]

    def flat(x):
        return x.reshape(-1, head_dim)

    def vmem(*shape):
        return pltpu.VMEM(shape, jnp.bfloat16)

    hbm = pl.BlockSpec(memory_space=pltpu.HBM)
    smem = pl.BlockSpec(memory_space=pltpu.SMEM)
    dma = pltpu.SemaphoreType.DMA
    wide = heads * BLK
    cached = cache_keys.shape[0] // BLK
    parts = rows // BLK
    out = pl.pallas_call(
        functools.partial(attend, n),
        out_shape=jax.ShapeDtypeStruct((parts, head_dim, wide), jnp.bfloat16),
        in_specs=[hbm] * 5 + [smem] * 4,
        out_specs=pl.BlockSpec(memory_space=pltpu.VMEM),
        scratch_shapes=[
            vmem(heads * rows, head_dim), vmem(wide, head_dim), vmem(wide, head_dim),
            vmem(cached, wide, head_dim), vmem(cached, wide, head_dim),
            vmem(heads, rows, head_dim), vmem(picked, 2, heads, BLK, head_dim),
            vmem(2, heads, BLK, head_dim), vmem(wide, wide), vmem(wide, wide),
            vmem(n, picked, 2, heads, BLK, head_dim),
            vmem(2, wide, head_dim), vmem(2, heads, BLK, head_dim),
            pltpu.VMEM((heads, head_dim, rows), jnp.float32),
            pltpu.VMEM((heads, 1, rows), jnp.float32),
            pltpu.VMEM((heads, 1, rows), jnp.float32),
            vmem(2, heads, 3 * BLK, rows), pltpu.VMEM((2, heads, 1, rows), jnp.float32),
            dma((n, 2, 2)), dma((n, 2)), dma((n, 2)), dma((n, 2)), dma((4,)), dma((5,)),
        ],
        compiler_params=pltpu.CompilerParams(
            collective_id=0, has_side_effects=True, vmem_limit_bytes=60 * 2**20),
    )(flat(queries), flat(new_keys), flat(new_values), cache_keys.reshape(cached, wide, head_dim),
      cache_values.reshape(cached, wide, head_dim),
      vertical_pool, vertical_lists, slash_lists, list_counts)
    flat_out = pl.pallas_call(
        functools.partial(restore, heads, groups),
        out_shape=jax.ShapeDtypeStruct((tokens * heads * groups, head_dim), jnp.bfloat16),
        in_specs=[hbm],
        out_specs=hbm,
        scratch_shapes=[vmem(parts, head_dim, wide), vmem(parts, wide, head_dim),
                        dma((parts,)), dma((parts,))],
        compiler_params=pltpu.CompilerParams(vmem_limit_bytes=60 * 2**20),
    )(out)
    return flat_out.reshape(tokens, heads, groups, head_dim)


def solution(mesh):
    in_specs = (
        P(("grp", "ctx"), "kvh", "sub", None),
        P(("grp", "ctx"), "kvh", None),
        P(("grp", "ctx"), "kvh", None),
        P(("grp", "ctx"), "kvh", None),
        P(("grp", "ctx"), "kvh", None),
        P(("grp", "ctx")),
        P(("grp", "ctx"), None),
        P(("grp", "ctx"), None),
        P(("grp", "ctx"), None),
    )
    out_specs = P(("grp", "ctx"), "kvh", "sub", None)
    return jax.shard_map(functools.partial(shards, mesh.shape["ctx"]), mesh=mesh,
                         in_specs=in_specs, out_specs=out_specs, check_vma=False)
```

```python
import functools
import math

import jax
import jax.numpy as jnp
from jax import lax
from jax.experimental import pallas as pl
from jax.experimental.pallas import tpu as pltpu
from jax.sharding import PartitionSpec as P

BLK = 128
MESH = pl.DeviceIdType.MESH


def attend(n, q_hbm, nk_hbm, nv_hbm, ck_hbm, cv_hbm, vp_ref, vl_ref, sl_ref, cnt_ref, o_ref,
           q_raw, nk_raw, nv_raw, ck_raw, cv_raw, q_ref, own_ref, new_ref, sort_kv, sort_q,
           pool, slash_raw, slash, acc, peak, total, rounded, fade,
           hop_send, hop_recv, sib_send, sib_recv, sl_sem, in_sem):
    z = lax.axis_index("ctx")
    s = lax.axis_index("sub")
    heads, rows, head_dim = q_ref.shape
    groups = rows // BLK
    wide = heads * BLK
    loads = [pltpu.make_async_copy(src, dst, in_sem.at[i]) for i, (src, dst) in enumerate(
        [(ck_hbm, ck_raw), (cv_hbm, cv_raw), (nk_hbm, nk_raw), (nv_hbm, nv_raw), (q_hbm, q_raw)])]
    loads[0].start()
    c = math.log2(math.e) / math.sqrt(head_dim)
    has_left = z > 0
    has_right = z < n - 1
    sib_id = {"sub": 1 - s}

    barrier = pltpu.get_barrier_semaphore()
    pl.semaphore_signal(barrier, inc=1, device_id=sib_id, device_id_type=MESH)

    @pl.when(has_left)
    def _():
        pl.semaphore_signal(barrier, inc=1, device_id={"ctx": z - 1}, device_id_type=MESH)

    @pl.when(has_right)
    def _():
        pl.semaphore_signal(barrier, inc=1, device_id={"ctx": z + 1}, device_id_type=MESH)

    ids = lax.broadcasted_iota(jnp.int32, (wide, wide), 0)
    at = lax.broadcasted_iota(jnp.int32, (wide, wide), 1)
    sort_kv[...] = jnp.where(at == (ids % BLK) * heads + ids // BLK, 1.0, 0.0).astype(jnp.bfloat16)
    token = (ids % BLK) // groups
    sort_q[...] = jnp.where(at == (token * heads + ids // BLK) * groups + ids % groups,
                            1.0, 0.0).astype(jnp.bfloat16)

    def by_head(raw):
        return jnp.dot(sort_kv[...], raw, preferred_element_type=jnp.float32).astype(jnp.bfloat16)

    def put_keys(dst, raw):
        ordered = by_head(raw)
        for h in range(heads):
            dst[h] = ordered[h * BLK:(h + 1) * BLK]

    def put_values(dst, raw):
        ordered = lax.dot_general(raw, sort_kv[...], (((0,), (1,)), ((), ())),
                                  preferred_element_type=jnp.float32).astype(jnp.bfloat16)
        for h in range(heads):
            dst[h] = ordered[:, h * BLK:(h + 1) * BLK]

    def chosen(cache, b):
        return cache[vp_ref[b]]

    pl.semaphore_wait(barrier, 1 + has_left.astype(jnp.int32) + has_right.astype(jnp.int32))

    def hop(src_ref, src, kv, right):
        return pltpu.make_async_remote_copy(
            src_ref=src_ref, dst_ref=pool.at[src, s, kv],
            send_sem=hop_send.at[src, int(right), kv], recv_sem=hop_recv.at[src, kv],
            device_id={"ctx": z + 1 if right else z - 1}, device_id_type=MESH)

    def sib(src, kv):
        return pltpu.make_async_remote_copy(
            src_ref=pool.at[src, s, kv], dst_ref=pool.at[src, s, kv],
            send_sem=sib_send.at[src, kv], recv_sem=sib_recv.at[src, kv],
            device_id=sib_id, device_id_type=MESH)

    def sib_in(src, kv):
        return pltpu.make_async_remote_copy(
            src_ref=pool.at[src, 1 - s, kv], dst_ref=pool.at[src, 1 - s, kv],
            send_sem=sib_send.at[src, kv], recv_sem=sib_recv.at[src, kv],
            device_id=sib_id, device_id_type=MESH)

    def slash_hop(src_ref=nk_hbm):
        return pltpu.make_async_remote_copy(
            src_ref=src_ref, dst_ref=slash_raw.at[s],
            send_sem=sl_sem.at[0], recv_sem=sl_sem.at[1],
            device_id={"ctx": z + 1}, device_id_type=MESH)

    def slash_sib(part):
        return pltpu.make_async_remote_copy(
            src_ref=slash_raw.at[part], dst_ref=slash_raw.at[part],
            send_sem=sl_sem.at[2], recv_sem=sl_sem.at[3],
            device_id=sib_id, device_id_type=MESH)

    for part, src_ref in enumerate((nk_hbm, nv_hbm)):
        @pl.when(has_right & (s == part))
        def _():
            slash_hop(src_ref).start()

    def send_own(kv):
        @pl.when(has_right)
        def _():
            hop(own_ref.at[s, kv], z, kv, True).start()

        @pl.when(has_left)
        def _():
            hop(own_ref.at[s, kv], z, kv, False).start()

    loads[0].wait()
    loads[1].start()
    put_keys(own_ref.at[s, 0], chosen(ck_raw, s))
    for load in loads[2:]:
        load.start()
    send_own(0)
    loads[1].wait()
    put_values(own_ref.at[s, 1], chosen(cv_raw, s))
    send_own(1)
    loads[2].wait()
    loads[3].wait()
    put_keys(new_ref.at[0], nk_raw[...])
    put_values(new_ref.at[1], nv_raw[...])
    put_keys(own_ref.at[1 - s, 0], chosen(ck_raw, 1 - s))
    put_values(own_ref.at[1 - s, 1], chosen(cv_raw, 1 - s))
    loads[4].wait()
    for part in range(rows // BLK):
        ordered = jnp.dot(sort_q[...], q_raw[part * wide:(part + 1) * wide],
                          preferred_element_type=jnp.float32).astype(jnp.bfloat16)
        for h in range(heads):
            q_ref[h, part * BLK:(part + 1) * BLK] = ordered[h * BLK:(h + 1) * BLK]

    def listed(slot):
        count = cnt_ref[0, 0]
        width = vl_ref.shape[1]
        if width <= 8:
            hit = jnp.int32(0)
            for i in range(width):
                hit = hit | jnp.where((vl_ref[0, i] == slot) & (i < count), 1, 0)
            return hit

        def one(i, hit):
            return hit | jnp.where((vl_ref[0, i] == slot) & (i < count), 1, 0)

        return lax.fori_loop(0, width, one, jnp.int32(0))

    def score(keys, q):
        return lax.dot_general(keys, q, (((1,), (1,)), ((), ())),
                               preferred_element_type=jnp.float32)

    def take_keys(side, blocks, first=False):
        for h in range(heads):
            q = q_ref[h]
            raw = []
            tops = []
            for keys, seen in blocks:
                scores = score(keys[h], q)
                if seen is None:
                    key_id = lax.broadcasted_iota(jnp.int32, scores.shape, 0)
                    row_id = lax.broadcasted_iota(jnp.int32, scores.shape, 1) // groups
                    scores = jnp.where(key_id <= row_id, scores, -jnp.inf)
                top = jnp.max(scores, axis=0, keepdims=True)
                if seen is not None:
                    top = jnp.where(seen > 0, top, -jnp.inf)
                raw.append(scores)
                tops.append(top)
            high = functools.reduce(jnp.maximum, tops)
            if not first:
                old = peak[h]
                high = jnp.maximum(old, high)
                factor = jnp.exp2((old - high) * c)
                fade[side, h] = factor
            peak[h] = high
            sums = []
            for i, ((_, seen), scores) in enumerate(zip(blocks, raw)):
                base = high if seen is None else jnp.where(seen > 0, high, jnp.inf)
                weights = jnp.exp2((scores - base) * c)
                sums.append(jnp.sum(weights, axis=0, keepdims=True))
                rounded[side, h, i * BLK:(i + 1) * BLK] = weights.astype(jnp.bfloat16)
            add = sum(sums[1:], sums[0])
            total[h] = add if first else total[h] * fade[side, h] + add

    def take_values(side, blocks, first=False):
        depth = len(blocks) * BLK
        for h in range(heads):
            values = jnp.concatenate([values[h] for values in blocks], 1)
            add = jnp.dot(values, rounded[side, h, :depth], preferred_element_type=jnp.float32)
            acc[h] = add if first else acc[h] * fade[side, h] + add

    take_keys(0, [(new_ref.at[0], None)]
              + [(own_ref.at[b, 0], listed(2 * z + b)) for b in range(2)], first=True)
    take_values(0, [new_ref.at[1]] + [own_ref.at[b, 1] for b in range(2)], first=True)

    @pl.when(has_left)
    def _():
        slash_hop().wait_recv()
        slash_sib(s).start()

    def arrive(src, kv, right):
        hop(own_ref.at[s, kv], src, kv, right).wait_recv()

        @pl.when(has_right if right else has_left)
        def _():
            hop(pool.at[src, s, kv], src, kv, right).start()

        sib(src, kv).start()

    def step(d, carry):
        sides = ((z + d, z + d < n, False), (z - d, z - d >= 0, True))
        for kv in range(2):
            for src, there, right in sides:
                @pl.when(there)
                def _():
                    arrive(src, kv, right)

            for side, (src, there, right) in enumerate(sides):
                @pl.when(there)
                def _():
                    sib_in(src, kv).wait_recv()
                    if kv == 0:
                        take_keys(side, [(pool.at[src, b, 0], listed(2 * src + b))
                                         for b in range(2)])
                    else:
                        take_values(side, [pool.at[src, b, 1] for b in range(2)])

        @pl.when((d == 1) & has_left)
        def _():
            slash_sib(1 - s).wait_recv()
            put_keys(slash.at[0], slash_raw[0])
            put_values(slash.at[1], slash_raw[1])
            back = jnp.int32(0)
            for i in range(sl_ref.shape[1]):
                back = back | jnp.where((sl_ref[0, i] == 1) & (i < cnt_ref[0, 1]), 1, 0)
            take_keys(0, [(slash.at[0], back)])
            take_values(0, [slash.at[1]])

        return carry

    lax.fori_loop(1, n, step, 0)

    for part in range(rows // BLK):
        lanes = slice(part * BLK, (part + 1) * BLK)
        done = jnp.concatenate(
            [(acc[h, :, lanes] / total[h, :, lanes]).astype(jnp.bfloat16) for h in range(heads)], 1)
        o_ref[part * wide:(part + 1) * wide] = lax.dot_general(
            sort_q[...], done, (((0,), (1,)), ((), ())),
            preferred_element_type=jnp.float32).astype(o_ref.dtype)

    def drain(src, carry):
        for kv in range(2):
            @pl.when(has_right & (src <= z))
            def _():
                hop(own_ref.at[s, kv], src, kv, True).wait_send()

            @pl.when(has_left & (src >= z))
            def _():
                hop(own_ref.at[s, kv], src, kv, False).wait_send()

            @pl.when(src != z)
            def _():
                sib(src, kv).wait_send()
        return carry

    lax.fori_loop(0, n, drain, 0)

    @pl.when(has_right)
    def _():
        slash_hop().wait_send()

    @pl.when(has_left)
    def _():
        slash_sib(s).wait_send()


def shards(n, queries, new_keys, new_values, cache_keys, cache_values,
           vertical_pool, vertical_lists, slash_lists, list_counts):
    tokens, heads, groups, head_dim = queries.shape
    rows = tokens * groups
    picked = vertical_pool.shape[0]

    def flat(x):
        return x.reshape(-1, head_dim)

    def vmem(*shape):
        return pltpu.VMEM(shape, jnp.bfloat16)

    hbm = pl.BlockSpec(memory_space=pltpu.HBM)
    smem = pl.BlockSpec(memory_space=pltpu.SMEM)
    dma = pltpu.SemaphoreType.DMA
    wide = heads * BLK
    cached = cache_keys.shape[0] // BLK
    out = pl.pallas_call(
        functools.partial(attend, n),
        out_shape=jax.ShapeDtypeStruct((tokens * heads * groups, head_dim), jnp.bfloat16),
        in_specs=[hbm] * 5 + [smem] * 4,
        out_specs=pl.BlockSpec(memory_space=pltpu.VMEM),
        scratch_shapes=[
            vmem(heads * rows, head_dim), vmem(wide, head_dim), vmem(wide, head_dim),
            vmem(cached, wide, head_dim), vmem(cached, wide, head_dim),
            vmem(heads, rows, head_dim), vmem(picked, 2, heads, BLK, head_dim),
            vmem(2, heads, BLK, head_dim), vmem(wide, wide), vmem(wide, wide),
            vmem(n, picked, 2, heads, BLK, head_dim),
            vmem(2, wide, head_dim), vmem(2, heads, BLK, head_dim),
            pltpu.VMEM((heads, head_dim, rows), jnp.float32),
            pltpu.VMEM((heads, 1, rows), jnp.float32),
            pltpu.VMEM((heads, 1, rows), jnp.float32),
            vmem(2, heads, 3 * BLK, rows), pltpu.VMEM((2, heads, 1, rows), jnp.float32),
            dma((n, 2, 2)), dma((n, 2)), dma((n, 2)), dma((n, 2)), dma((4,)), dma((5,)),
        ],
        compiler_params=pltpu.CompilerParams(
            collective_id=0, has_side_effects=True, vmem_limit_bytes=60 * 2**20),
    )(flat(queries), flat(new_keys), flat(new_values), cache_keys.reshape(cached, wide, head_dim),
      cache_values.reshape(cached, wide, head_dim),
      vertical_pool, vertical_lists, slash_lists, list_counts)
    return out.reshape(tokens, heads, groups, head_dim)


def solution(mesh):
    in_specs = (
        P(("grp", "ctx"), "kvh", "sub", None),
        P(("grp", "ctx"), "kvh", None),
        P(("grp", "ctx"), "kvh", None),
        P(("grp", "ctx"), "kvh", None),
        P(("grp", "ctx"), "kvh", None),
        P(("grp", "ctx")),
        P(("grp", "ctx"), None),
        P(("grp", "ctx"), None),
        P(("grp", "ctx"), None),
    )
    out_specs = P(("grp", "ctx"), "kvh", "sub", None)
    return jax.shard_map(functools.partial(shards, mesh.shape["ctx"]), mesh=mesh,
                         in_specs=in_specs, out_specs=out_specs, check_vma=False)
```
